32 devices in a mesh: frame: 4 (over x, core), tile: 8 (over z, y).
Axes of the slice: x: 2, y: 2, z: 4, core: 2. Of those that a mesh axis runs over, the one named last changes fastest.
Arguments:
- frames: bfloat16 [4, 64, 64, 2048], P('frame', None, 'tile'), may hold values from -6 to 6
- predict_w: bfloat16 [2, 4, 3, 3, 64, 64], replicated, may hold values from -0.25 to 0.25
- predict_b: float32 [2, 4, 64], replicated, may hold values from -2 to 2
- update_w: bfloat16 [2, 4, 3, 3, 64, 64], replicated, may hold values from -0.25 to 0.25
- update_b: float32 [2, 4, 64], replicated, may hold values from -2 to 2
Outputs:
- coefficients: bfloat16 [4, 64, 64, 2048], P('frame', None, 'tile')
The draws below stay inside these ranges and needn't reach their ends.
All inputs are finite; a program needn't handle non-finite values.
Results may differ from the reference program's by a relative error of at most 0.009.
Values may be sent and summed in bfloat16 or wider, within the bound.
A program may use at most 128 MiB of HBM per device.

```python
import jax
import jax.numpy as jnp
from jax import lax

C = 64
W = 2048
LAYERS = 4
FRAMES = 4
H = 64


def shard_levels(own_key, dims, shards, low, top_value):
    loudness, own = 1.0, jax.random.fold_in(own_key, 6)
    for dim, blocks in shards:
        heights = jnp.exp(jax.random.uniform(jax.random.fold_in(own, dim), (blocks,), jnp.float32, low / len(shards), top_value / len(shards)))
        loudness = loudness * jnp.repeat(heights, dims[dim] // blocks).reshape([-1 if axis == dim else 1 for axis in range(len(dims))])
    return loudness


def normal_values(stream_key, dims, width, reach, cuts=(), held_as=jnp.bfloat16):
    array = jax.random.normal(stream_key, dims, jnp.float32) * width
    if len(cuts) > 0:
        array = shard_levels(stream_key, dims, cuts, -0.22, 0.18) * array
    return jnp.clip(array, min=-reach, max=reach).astype(held_as)


def setup_inputs(seed: int = 0) -> dict:
    keys = jax.random.split(jax.random.key(seed), 6)
    return {
        "frames": normal_values(keys[0], (FRAMES, C, H, W), 1.0, 6.0, ((0, 4), (2, 8))),
        "predict_w": normal_values(keys[1], (2, LAYERS, 3, 3, C, C), (9 * C) ** -0.5, 0.25),
        "predict_b": normal_values(keys[2], (2, LAYERS, C), 0.3, 2.0, (), jnp.float32),
        "update_w": normal_values(keys[3], (2, LAYERS, 3, 3, C, C), (9 * C) ** -0.5, 0.25),
        "update_b": normal_values(keys[4], (2, LAYERS, C), 0.3, 2.0, (), jnp.float32),
    }


def conv_layer(field, kernel, bias_row):
    weights = jnp.transpose(kernel.astype(jnp.float32), (2, 3, 0, 1))
    result = lax.conv_general_dilated(field, weights, (1, 1), ((1, 1), (1, 1)), dimension_numbers=("NCHW", "OIHW", "NCHW"), precision=lax.Precision.HIGHEST)
    return result + bias_row[None, :, None, None]


def network(field, kernels, biases):
    hidden = field.astype(jnp.float32)
    for layer_index in range(LAYERS):
        result = conv_layer(hidden, kernels[layer_index], biases[layer_index])
        if layer_index < LAYERS - 1:
            rounded = lax.optimization_barrier(jnp.maximum(result, 0.0).astype(jnp.bfloat16))
            hidden = rounded.astype(jnp.float32)
    return result


def reference(frames, predict_w, predict_b, update_w, update_b):
    even_frames = frames[0::2]
    odd_frames = frames[1::2]
    high_one = (odd_frames.astype(jnp.float32) - network(even_frames, predict_w[0], predict_b[0])).astype(jnp.bfloat16)
    low_one = (even_frames.astype(jnp.float32) + network(high_one, update_w[0], update_b[0])).astype(jnp.bfloat16)
    low_even = low_one[0::2]
    low_odd = low_one[1::2]
    high_two = (low_odd.astype(jnp.float32) - network(low_even, predict_w[1], predict_b[1])).astype(jnp.bfloat16)
    low_two = (low_even.astype(jnp.float32) + network(high_two, update_w[1], update_b[1])).astype(jnp.bfloat16)
    stacked = jnp.stack([low_two, high_one[0::2], high_two, high_one[1::2]], axis=1)
    return stacked.reshape(frames.shape)
```

```python
import functools

import jax
import jax.numpy as jnp
from jax import lax
from jax.experimental import pallas as pl
from jax.experimental.pallas import tpu as pltpu
from jax.sharding import PartitionSpec as P

LANES = 128
HALF_LANES = LANES // 2
PEERS = ((0, 1), (1, 0), (1, 1), (0, 0))
EDGES = ("e0", "e1", "h0", "h1", "f", "g")
RECV, SEND = {}, {}
for _kind in ("main", "pad"):
    for _c in range(2):
        for _dx in range(2):
            RECV[_kind, _c, _dx] = len(RECV)
for _k in range(8):
    RECV["out", _k] = len(RECV)
for _e in EDGES:
    for _side in ("inner", "outer"):
        RECV[_e, _side] = len(RECV)
for _kind in ("main", "pad"):
    for _p in PEERS:
        SEND[_kind, _p] = len(SEND)
for _name in ("high0", "high1", "high2", "low2"):
    for _k in range(2):
        SEND[_name, _k] = len(SEND)
for _e in EDGES:
    for _side in ("inner", "outer"):
        SEND[_e, _side] = len(SEND)


def flip(v, d):
    return v + d - 2 * v * d


def kernel(tiles, own, pw, uw, pb, ub, out, e, o, h, fb, g2, l2, a_ref, c_ref, d_ref, acc0, acc1, wa, wb, wc, wd,
           bias, cuts, pads, send_sem, recv_sem, local_sem):
    rows, channels, width = own.shape
    layers = pw.shape[1]
    block = width // 4
    span = block + LANES
    edge = rows // 2
    f = lax.axis_index("frame")
    t = lax.axis_index("tile")
    core, x = lax.rem(f, 2), lax.div(f, 2)
    y, slab = lax.rem(t, 2), lax.div(t, 2)
    slabs = tiles // 2
    first_tile = t - y
    partner = f + 1 - 2 * core
    q = 2 * x + y
    is_even, is_odd = core == 0, core == 1
    outer_slab = slab + 2 * core - 1
    has_outer = jnp.logical_and(outer_slab >= 0, outer_slab < slabs)
    outer_tile = t + 4 * core - 2
    me_local = y == core

    def cols(k, size=block):
        return pl.ds(pl.multiple_of(k * block, LANES), size)

    barrier = pltpu.get_barrier_semaphore()

    def greet(frame, tile):
        pl.semaphore_signal(
            barrier, inc=1, device_id={"frame": frame, "tile": tile}, device_id_type=pl.DeviceIdType.MESH,
        )

    for dx in range(2):
        for dc in range(2):
            for dy in range(2):
                if dx or dc or dy:
                    greet(2 * flip(x, dx) + flip(core, dc), first_tile + flip(y, dy))

    @pl.when(has_outer)
    def _():
        greet(partner, outer_tile)

    def remote(src, dst, send, recv, frame, tile):
        return pltpu.make_async_remote_copy(
            src_ref=src, dst_ref=dst, send_sem=send_sem.at[send], recv_sem=recv_sem.at[recv],
            device_id={"frame": frame, "tile": tile}, device_id_type=pl.DeviceIdType.MESH,
        )

    cut_copies = [
        pltpu.make_async_copy(
            own.at[:, :, k * block + block - LANES : k * block + block + LANES], cuts.at[k], local_sem.at[k]
        )
        for k in range(3)
    ]
    for copy in cut_copies:
        copy.start()

    @pl.when(jnp.logical_not(has_outer))
    def _():
        zero = jnp.zeros((edge, channels, span), jnp.bfloat16)
        at = pl.ds(3 * edge * core, edge)
        for v in range(3):
            for d in range(2):
                e[v, d, at] = zero
                h[v, d, at] = zero
            fb[0, v, at] = zero
            g2[v, at] = zero

    pl.semaphore_wait(barrier, 7 + has_outer.astype(jnp.int32))

    mine = slice(edge, edge + rows)

    def landing(c, dx, part):
        at = slice(0, block) if part == "main" else slice(block, span)
        return e.at[1, dx, mine, :, at] if c == 0 else o.at[dx, :, :, at]

    def parcel(c, peer, part):
        dx, dy = peer
        px, py = flip(x, dx), flip(y, dy)
        pq = 2 * px + py
        src = own.at[:, :, cols(pq)] if part == "main" else pads.at[pq]
        return src, landing(c, dx, part), 2 * px + y, first_tile + py

    def ship(c, peer, part, action):
        src, dst, frame, tile = parcel(c, peer, part)
        copy = remote(src, dst, SEND[part, peer], RECV[part, c, peer[0]], frame, tile)
        if peer != (0, 0):
            action(copy)
        else:
            same = y == c

            @pl.when(jnp.logical_not(same))
            def _():
                action(copy)

            @pl.when(same)
            def _():
                action(pltpu.make_async_copy(src, dst, local_sem.at[3 if part == "main" else 4]))

    def start(copy):
        copy.start()

    def settle(copy):
        if copy.is_remote:
            copy.wait_send()

    def arrive(c, dx):
        for part in ("main", "pad"):
            src, dst, frame, tile = parcel(c, (dx, 0), part)
            copy = remote(src, dst, SEND[part, (dx, 0)], RECV[part, c, dx], frame, tile)
            if dx:
                copy.wait_recv()
            else:
                local = jnp.logical_and(me_local, core == c)

                @pl.when(jnp.logical_not(local))
                def _(copy=copy):
                    copy.wait_recv()

                @pl.when(local)
                def _(src=src, dst=dst, part=part):
                    pltpu.make_async_copy(src, dst, local_sem.at[3 if part == "main" else 4]).wait()

    @pl.when(is_even)
    def _():
        for peer in ((0, 1), (1, 0), (0, 0)):
            ship(0, peer, "main", start)

    @pl.when(is_odd)
    def _():
        ship(1, (0, 0), "main", start)

    lane = lax.broadcasted_iota(jnp.int32, (1, 1, LANES), 2)
    for copy in cut_copies:
        copy.wait()
    nothing = jnp.zeros((rows, channels, LANES), jnp.float32)
    for k in range(4):
        right = cuts[k, :, :, LANES:].astype(jnp.float32) if k < 3 else nothing
        left = cuts[k - 1, :, :, :LANES].astype(jnp.float32) if k > 0 else nothing
        pads[k] = jnp.where(lane < HALF_LANES, right, left).astype(jnp.bfloat16)

    @pl.when(is_even)
    def _():
        for peer in ((0, 1), (1, 0), (0, 0)):
            ship(0, peer, "pad", start)
        for part in ("main", "pad"):
            ship(0, (1, 1), part, start)

    @pl.when(is_odd)
    def _():
        ship(1, (0, 0), "pad", start)

    def build(k_ref, level, w_ref):
        for layer in range(layers):
            w_ref[layer] = jnp.zeros(w_ref.shape[1:], w_ref.dtype)
            for p in range(2):
                for s in range(3):
                    for r in range(3):
                        at = 4 * channels * s + channels * (r + p)
                        w_ref[layer, p * channels : (p + 1) * channels, at : at + channels] = k_ref[level, layer, r, s]

    def spread_bias(b_ref, level, base):
        row = lax.broadcasted_iota(jnp.int32, (channels, channels), 0)
        col = lax.broadcasted_iota(jnp.int32, (channels, channels), 1)
        for layer in range(layers):
            values = jnp.where(row == col, b_ref[level, layer : layer + 1, :], 0.0)
            column = jnp.sum(values, axis=1, keepdims=True)
            full = jnp.broadcast_to(column, (channels, LANES))
            bias[base + layer, :channels] = full
            bias[base + layer, channels:] = full

    for k, (k_ref, b_ref, level, w_ref) in enumerate(
        ((pw, pb, 0, wa), (uw, ub, 0, wb), (pw, pb, 1, wc), (uw, ub, 1, wd))
    ):
        build(k_ref, level, w_ref)
        spread_bias(b_ref, level, k * layers)
    arrive(0, 0)

    @pl.when(is_odd)
    def _():
        for peer in ((0, 1), (1, 0), (1, 1)):
            for part in ("main", "pad"):
                ship(1, peer, part, start)

    lane2 = lax.broadcasted_iota(jnp.int32, (1, LANES), 1)
    in_frame = jnp.logical_or(
        jnp.logical_and(lane2 < HALF_LANES, q < 3), jnp.logical_and(lane2 >= HALF_LANES, q > 0)
    )

    def clip(value):
        return jnp.concatenate([value[:, :block], jnp.where(in_frame, value[:, block:], 0.0)], axis=1)

    def step(index):
        return 0 if index is None else 2 * index

    def edge_copy(name, side, field, index):
        if side == "inner":
            src, dst, tile = edge * (2 - core), 3 * edge * core, t
        else:
            src, dst, tile = edge * (1 + core), 3 * edge * (1 - core), outer_tile
        lead = (1,) if index is None else (1, index)
        return remote(
            field.at[lead + (pl.ds(src, edge),)], field.at[lead + (pl.ds(dst, edge),)],
            SEND[name, side] + step(index), RECV[name, side] + step(index), partner, tile,
        )

    def edge_in(name, side, field, index):
        if side == "inner":
            at, tile = 3 * edge * (1 - core), t
        else:
            at, tile = 3 * edge * core, outer_tile
        lead = (1,) if index is None else (1, index)
        piece = field.at[lead + (pl.ds(at, edge),)]
        return remote(piece, piece, SEND[name, side] + step(index), RECV[name, side] + step(index), partner, tile), at

    def send_edge(name, side, field, index=None):
        if side == "inner":
            edge_copy(name, side, field, index).start()
        else:
            @pl.when(has_outer)
            def _():
                edge_copy(name, side, field, index).start()

    def edge_sent(name, field, index=None):
        edge_copy(name, "inner", field, index).wait_send()

        @pl.when(has_outer)
        def _():
            edge_copy(name, "outer", field, index).wait_send()

    def turn(field, lead, at, count):
        for k in range(count):
            value = field[(1,) + lead + (at + k,)]
            field[(0,) + lead + (at + k,)] = pltpu.roll(value, 1, 1)
            field[(2,) + lead + (at + k,)] = pltpu.roll(value, span - 1, 1)

    hidden = (a_ref, c_ref, d_ref)

    def run_steps(steps):
        accs = (acc0, acc1)
        waiting = None
        for k, (mm, post, layer, offset) in enumerate(steps):
            if waiting is not None and waiting[1] < layer and waiting[2] < offset + 6 and offset < waiting[2] + 4:
                waiting[0](accs[(k - 1) % 2])
                waiting = None
            mm(accs[k % 2])
            if waiting is not None:
                waiting[0](accs[(k - 1) % 2])
            waiting = post, layer, offset
        waiting[0](accs[(len(steps) - 1) % 2])

    def network(read, w_ref, base, finish, outer_phase):
        steps = []
        for layer in range(layers):
            total = 2 * rows - 2 * (layer + 1)
            last = layer == layers - 1
            if outer_phase:
                count, begin = edge, core * (total - edge)
            else:
                count, begin = total - edge, edge * (1 - core)
            offsets = sorted({min(k, count - 4) for k in range(0, count, 4)})
            source = read if layer == 0 else (lambda s, at, ref=hidden[layer - 1]: ref[s, at])
            for offset in offsets:
                j = begin + offset

                def mm(acc, j=j, source=source, layer=layer):
                    parts = []
                    for s in range(3):
                        parts.append(jnp.concatenate(
                            [source(s, pl.ds(j + 2 * k, 4)).reshape(4 * channels, span) for k in range(2)], axis=1
                        ))
                    stack = jnp.concatenate(parts, axis=0)
                    acc[...] = jnp.dot(w_ref[layer], stack, preferred_element_type=jnp.float32)

                def post(acc, j=j, layer=layer, last=last):
                    shift = jnp.concatenate([bias[base + layer]] * (span // LANES), axis=1)
                    for k in range(2):
                        value = acc[:, k * span : (k + 1) * span] + shift
                        if last:
                            finish(j + 2 * k, value)
                            continue
                        value = jnp.maximum(value, 0.0)
                        if outer_phase:
                            halves = []
                            for p in range(2):
                                i = 2 * k + p
                                outside = jnp.logical_and(
                                    jnp.logical_not(has_outer),
                                    jnp.logical_or(
                                        jnp.logical_and(is_even, i < layers - 1 - layer),
                                        jnp.logical_and(is_odd, i > layer),
                                    ),
                                )
                                halves.append(jnp.where(outside, 0.0, value[p * channels : (p + 1) * channels]))
                            value = jnp.concatenate(halves, axis=0)
                        emit(hidden[layer], (), j + 2 * k, value)

                steps.append((mm, post, layer, offset))
        run_steps(steps)

    def emit(ref, lead, j, value, versions=(0, 1, 2)):
        packed = clip(value).astype(jnp.bfloat16)
        for v in versions:
            turned = packed if v == 1 else pltpu.roll(packed, 1 if v == 0 else span - 1, 1)
            for p in range(2):
                ref[(v,) + lead + (j + p,)] = turned[p * channels : (p + 1) * channels]

    def pair_of(values):
        return jnp.concatenate([values[0], values[1]], axis=0).astype(jnp.float32)

    def field_network(name, field, index, w_ref, base, finish, after_inner):
        lead = () if index is None else (index,)
        read = lambda s, at: field[(s,) + lead + (at,)]
        copy, at = edge_in(name, "inner", field, index)
        copy.wait_recv()
        turn(field, lead, at, edge)
        network(read, w_ref, base, finish, False)
        after_inner()
        copy, at = edge_in(name, "outer", field, index)

        @pl.when(has_outer)
        def _():
            copy.wait_recv()
            turn(field, lead, at, edge)

        network(read, w_ref, base, finish, True)

    def out_copy(name, half, source, frame, dx, d):
        at = edge * (1 - core) if half == 0 else edge * core
        dy = flip(y, core)
        src = source(at)
        dst = out.at[pl.ds(at, edge), :, cols(q)]
        return remote(src, dst, SEND[name, half] + 2 * d, RECV["out", 0] + 4 * dx + 2 * dy + half, frame, first_tile + core), (
            lambda: pltpu.make_async_copy(src, dst, local_sem.at[5 + half])
        )

    def deliver(name, half, source, frame, dx, action, d=0):
        copy, local = out_copy(name, half, source, frame, dx, d)
        mine_only = jnp.logical_and(f == frame, me_local)

        @pl.when(jnp.logical_not(mine_only))
        def _():
            action(copy)

        @pl.when(mine_only)
        def _():
            action(local())

    def high_piece(d):
        return lambda at: h.at[1, d, pl.ds(edge + at, edge), :, 0:block]

    turn(e, (0,), edge, rows)
    send_edge("e0", "inner", e, 0)
    send_edge("e0", "outer", e, 0)
    def pair_network(d, carry):
        p_index = flip(x, d)

        @pl.when(d == 1)
        def _():
            arrive(0, 1)
            send_edge("e0", "inner", e, d)
            send_edge("e0", "outer", e, d)
            turn(e, (d,), edge, rows)

        def high(j, value):
            old = pair_of([o[d, j], o[d, j + 1]])
            emit(h, (d,), edge + j, old - value)

        def high_inner():
            send_edge("h0", "inner", h, d)
            deliver("high0", 0, high_piece(d), 2 * p_index + 1, d, start, d)

        for dx in range(2):
            @pl.when(d == dx)
            def _(dx=dx):
                arrive(1, dx)

        field_network("e0", e, d, wa, 0, high, high_inner)
        send_edge("h0", "outer", h, d)
        deliver("high0", 1, high_piece(d), 2 * p_index + 1, d, start, d)

        def low(j, value):
            old = pair_of([e[1, d, edge + j], e[1, d, edge + j + 1]])
            packed = clip(old + value).astype(jnp.bfloat16)
            for v in range(3):
                turned = packed if v == 1 else pltpu.roll(packed, 1 if v == 0 else span - 1, 1)
                for p in range(2):
                    fb[p_index, v, edge + j + p] = turned[p * channels : (p + 1) * channels]

        def low_inner():
            @pl.when(x == d)
            def _():
                send_edge("f", "inner", fb.at[0])

        field_network("h0", h, d, wb, layers, low, low_inner)

        @pl.when(x == d)
        def _():
            send_edge("f", "outer", fb.at[0])

        return carry

    lax.fori_loop(0, 2, pair_network, 0)

    def high_two(j, value):
        old = pair_of([fb[1, 1, edge + j], fb[1, 1, edge + j + 1]])
        emit(g2, (), edge + j, old - value)

    def g_piece(at):
        return g2.at[1, pl.ds(edge + at, edge), :, 0:block]

    def g_inner():
        send_edge("g", "inner", g2)
        deliver("high2", 0, g_piece, 2, 1 - x, start)

    field_network("f", fb.at[0], None, wc, 2 * layers, high_two, g_inner)
    send_edge("g", "outer", g2)
    deliver("high2", 1, g_piece, 2, 1 - x, start)

    def low_two(j, value):
        old = pair_of([fb[0, 1, edge + j], fb[0, 1, edge + j + 1]])
        packed = (old + value)[:, :block].astype(jnp.bfloat16)
        for p in range(2):
            l2[j + p] = packed[p * channels : (p + 1) * channels]

    def l_piece(at):
        return l2.at[pl.ds(at, edge)]

    def l_inner():
        deliver("low2", 0, l_piece, 0, x, start)

    field_network("g", g2, None, wd, 3 * layers, low_two, l_inner)
    deliver("low2", 1, l_piece, 0, x, start)

    for dx in range(2):
        for dy in range(2):
            for half in range(2):
                rows_at = edge * (1 - y) if half == 0 else edge * y
                dst = out.at[pl.ds(rows_at, edge), :, cols(2 * flip(x, dx) + flip(y, dy))]
                copy = remote(dst, dst, 0, RECV["out", 0] + 4 * dx + 2 * dy + half, partner, t)
                if dx or dy:
                    copy.wait_recv()
                else:
                    @pl.when(jnp.logical_not(me_local))
                    def _(copy=copy):
                        copy.wait_recv()

                    @pl.when(me_local)
                    def _(dst=dst, half=half):
                        pltpu.make_async_copy(dst, dst, local_sem.at[5 + half]).wait()

    for c, flag in ((0, is_even), (1, is_odd)):
        @pl.when(flag)
        def _(c=c):
            for peer in PEERS:
                for part in ("main", "pad"):
                    ship(c, peer, part, settle)
    for d in range(2):
        edge_sent("e0", e, d)
        edge_sent("h0", h, d)
        for half in range(2):
            deliver("high0", half, high_piece(d), 2 * flip(x, d) + 1, d, settle, d)
    edge_sent("f", fb.at[0])
    edge_sent("g", g2)
    for half in range(2):
        deliver("high2", half, g_piece, 2, 1 - x, settle)
        deliver("low2", half, l_piece, 0, x, settle)


def local(frames, predict_w, predict_b, update_w, update_b):
    own = jnp.transpose(frames[0], (1, 0, 2))
    rows, channels, width = own.shape
    layers = predict_w.shape[1]
    block = width // 4
    span = block + LANES
    tiles = lax.axis_size("tile")
    vmem = pl.BlockSpec(memory_space=pltpu.VMEM)
    hbm = pl.BlockSpec(memory_space=pl.ANY)

    def buffer(*lead, columns=span):
        return pltpu.VMEM(lead + (channels, columns), jnp.bfloat16)

    weight = pltpu.VMEM((layers, 2 * channels, 12 * channels), jnp.bfloat16)
    acc = pltpu.VMEM((2 * channels, 2 * span), jnp.float32)
    result = pl.pallas_call(
        functools.partial(kernel, tiles),
        out_shape=jax.ShapeDtypeStruct(own.shape, jnp.bfloat16),
        in_specs=[hbm, vmem, vmem, vmem, vmem],
        out_specs=hbm,
        scratch_shapes=[
            buffer(3, 2, 2 * rows), buffer(2, rows), buffer(3, 2, 2 * rows), buffer(2, 3, 2 * rows),
            buffer(3, 2 * rows), buffer(rows, columns=block),
            buffer(3, 2 * rows - 2), buffer(3, 2 * rows - 4), buffer(3, 2 * rows - 6),
            acc, acc, weight, weight, weight, weight,
            pltpu.VMEM((4 * layers, 2 * channels, LANES), jnp.float32),
            buffer(3, rows, columns=2 * LANES), buffer(4, rows, columns=LANES),
            pltpu.SemaphoreType.DMA((len(SEND),)),
            pltpu.SemaphoreType.DMA((len(RECV),)),
            pltpu.SemaphoreType.DMA((7,)),
        ],
        compiler_params=pltpu.CompilerParams(
            collective_id=0, has_side_effects=True, vmem_limit_bytes=60 * 1024 * 1024
        ),
    )(own, predict_w, update_w, predict_b, update_b)
    return jnp.transpose(result, (1, 0, 2))[None]


def solution(mesh):
    in_specs = (P("frame", None, "tile", None), P(), P(), P(), P())
    out_specs = P("frame", None, "tile", None)
    return jax.shard_map(local, mesh=mesh, in_specs=in_specs, out_specs=out_specs, check_vma=False)
```

```python
import functools

import jax
import jax.numpy as jnp
from jax import lax
from jax.experimental import pallas as pl
from jax.experimental.pallas import tpu as pltpu
from jax.sharding import PartitionSpec as P

LANES = 128
HALF_LANES = LANES // 2
PEERS = ((0, 1), (1, 0), (1, 1), (0, 0))
EDGES = ("e0", "e1", "h0", "h1", "f", "g")
RECV, SEND = {}, {}
for _kind in ("main", "pad"):
    for _c in range(2):
        for _dx in range(2):
            RECV[_kind, _c, _dx] = len(RECV)
for _k in range(8):
    RECV["out", _k] = len(RECV)
for _e in EDGES:
    for _side in ("inner", "outer"):
        RECV[_e, _side] = len(RECV)
for _kind in ("main", "pad"):
    for _p in PEERS:
        SEND[_kind, _p] = len(SEND)
for _name in ("high0", "high1", "high2", "low2"):
    for _k in range(2):
        SEND[_name, _k] = len(SEND)
for _e in EDGES:
    for _side in ("inner", "outer"):
        SEND[_e, _side] = len(SEND)


def flip(v, d):
    return v + d - 2 * v * d


def kernel(tiles, own, pw, uw, pb, ub, out, e, o, h, fb, g2, l2, a_ref, c_ref, d_ref, acc0, acc1, wa, wb, wc, wd,
           bias, cuts, pads, packs, send_sem, recv_sem, local_sem):
    rows, channels, width = own.shape
    layers = pw.shape[1]
    block = width // 4
    span = block + LANES
    edge = rows // 2
    f = lax.axis_index("frame")
    t = lax.axis_index("tile")
    core, x = lax.rem(f, 2), lax.div(f, 2)
    y, slab = lax.rem(t, 2), lax.div(t, 2)
    slabs = tiles // 2
    first_tile = t - y
    partner = f + 1 - 2 * core
    q = 2 * x + y
    is_even, is_odd = core == 0, core == 1
    outer_slab = slab + 2 * core - 1
    has_outer = jnp.logical_and(outer_slab >= 0, outer_slab < slabs)
    outer_tile = t + 4 * core - 2
    me_local = y == core

    def cols(k, size=block):
        return pl.ds(pl.multiple_of(k * block, LANES), size)

    barrier = pltpu.get_barrier_semaphore()

    def greet(frame, tile):
        pl.semaphore_signal(
            barrier, inc=1, device_id={"frame": frame, "tile": tile}, device_id_type=pl.DeviceIdType.MESH,
        )

    for dx in range(2):
        for dc in range(2):
            for dy in range(2):
                if dx or dc or dy:
                    greet(2 * flip(x, dx) + flip(core, dc), first_tile + flip(y, dy))

    @pl.when(has_outer)
    def _():
        greet(partner, outer_tile)

    def remote(src, dst, send, recv, frame, tile):
        return pltpu.make_async_remote_copy(
            src_ref=src, dst_ref=dst, send_sem=send_sem.at[send], recv_sem=recv_sem.at[recv],
            device_id={"frame": frame, "tile": tile}, device_id_type=pl.DeviceIdType.MESH,
        )

    cut_copies = [
        pltpu.make_async_copy(
            own.at[:, :, k * block + block - LANES : k * block + block + LANES], cuts.at[k], local_sem.at[k]
        )
        for k in range(3)
    ]
    for copy in cut_copies:
        copy.start()

    @pl.when(jnp.logical_not(has_outer))
    def _():
        zero = jnp.zeros((edge, channels, span), jnp.bfloat16)
        at = pl.ds(3 * edge * core, edge)
        for v in range(3):
            for d in range(2):
                e[v, d, at] = zero
                h[v, d, at] = zero
            fb[0, v, at] = zero
            g2[v, at] = zero

    pl.semaphore_wait(barrier, 7 + has_outer.astype(jnp.int32))

    mine = slice(edge, edge + rows)
    reach = 4 * layers
    group = LANES // (2 * reach)

    def landing(c, dx, part):
        if part == "pad":
            return packs.at[c, dx]
        return e.at[1, dx, mine, :, 0:block] if c == 0 else o.at[dx, :, :, 0:block]

    def parcel(c, peer, part):
        dx, dy = peer
        px, py = flip(x, dx), flip(y, dy)
        pq = 2 * px + py
        src = own.at[:, :, cols(pq)] if part == "main" else pads.at[pq]
        return src, landing(c, dx, part), 2 * px + y, first_tile + py

    def ship(c, peer, part, action):
        src, dst, frame, tile = parcel(c, peer, part)
        copy = remote(src, dst, SEND[part, peer], RECV[part, c, peer[0]], frame, tile)
        if peer != (0, 0):
            action(copy)
        else:
            same = y == c

            @pl.when(jnp.logical_not(same))
            def _():
                action(copy)

            @pl.when(same)
            def _():
                action(pltpu.make_async_copy(src, dst, local_sem.at[3 if part == "main" else 4]))

    def start(copy):
        copy.start()

    def settle(copy):
        if copy.is_remote:
            copy.wait_send()

    def arrive(c, dx):
        for part in ("main", "pad"):
            src, dst, frame, tile = parcel(c, (dx, 0), part)
            copy = remote(src, dst, SEND[part, (dx, 0)], RECV[part, c, dx], frame, tile)
            if dx:
                copy.wait_recv()
            else:
                local = jnp.logical_and(me_local, core == c)

                @pl.when(jnp.logical_not(local))
                def _(copy=copy):
                    copy.wait_recv()

                @pl.when(local)
                def _(src=src, dst=dst, part=part):
                    pltpu.make_async_copy(src, dst, local_sem.at[3 if part == "main" else 4]).wait()
        for unit in range(rows // group):
            value = packs[c, dx, unit].astype(jnp.float32)
            for i in range(group):
                strip = pltpu.roll(value, (-reach - 2 * reach * i) % LANES, 1)
                strip = jnp.where(jnp.logical_or(lane < reach, lane >= LANES - reach), strip, 0.0).astype(jnp.bfloat16)
                row = unit * group + i
                if c == 0:
                    e[1, dx, edge + row, :, block:span] = strip
                else:
                    o[dx, row, :, block:span] = strip

    @pl.when(is_even)
    def _():
        for peer in ((0, 1), (1, 0), (0, 0)):
            ship(0, peer, "main", start)

    @pl.when(is_odd)
    def _():
        for peer in ((0, 1), (1, 0), (0, 0)):
            ship(1, peer, "main", start)

    lane = lax.broadcasted_iota(jnp.int32, (1, LANES), 1)
    for copy in cut_copies:
        copy.wait()
    for k in range(4):
        for unit in range(rows // group):
            total = jnp.zeros((channels, LANES), jnp.float32)
            for i in range(group):
                row = unit * group + i
                strip = jnp.zeros((channels, LANES), jnp.float32)
                if k < 3:
                    strip = jnp.where(lane < reach, cuts[k, row, :, LANES:].astype(jnp.float32), strip)
                if k > 0:
                    strip = jnp.where(lane >= LANES - reach, cuts[k - 1, row, :, :LANES].astype(jnp.float32), strip)
                total = total + pltpu.roll(strip, (reach + 2 * reach * i) % LANES, 1)
            pads[k, unit] = total.astype(jnp.bfloat16)

    @pl.when(is_even)
    def _():
        for peer in ((0, 1), (1, 0), (0, 0)):
            ship(0, peer, "pad", start)
        for part in ("main", "pad"):
            ship(0, (1, 1), part, start)

    @pl.when(is_odd)
    def _():
        for peer in ((0, 1), (1, 0), (0, 0)):
            ship(1, peer, "pad", start)
        for part in ("main", "pad"):
            ship(1, (1, 1), part, start)

    def build(k_ref, level, w_ref):
        for layer in range(layers):
            w_ref[layer] = jnp.zeros(w_ref.shape[1:], w_ref.dtype)
            for p in range(2):
                for s in range(3):
                    for r in range(3):
                        at = 4 * channels * s + channels * (r + p)
                        w_ref[layer, p * channels : (p + 1) * channels, at : at + channels] = k_ref[level, layer, r, s]

    def spread_bias(b_ref, level, base):
        row = lax.broadcasted_iota(jnp.int32, (channels, channels), 0)
        col = lax.broadcasted_iota(jnp.int32, (channels, channels), 1)
        for layer in range(layers):
            values = jnp.where(row == col, b_ref[level, layer : layer + 1, :], 0.0)
            column = jnp.sum(values, axis=1, keepdims=True)
            full = jnp.broadcast_to(column, (channels, LANES))
            bias[base + layer, :channels] = full
            bias[base + layer, channels:] = full

    for k, (k_ref, b_ref, level, w_ref) in enumerate(
        ((pw, pb, 0, wa), (uw, ub, 0, wb), (pw, pb, 1, wc), (uw, ub, 1, wd))
    ):
        build(k_ref, level, w_ref)
        spread_bias(b_ref, level, k * layers)
    arrive(0, 0)

    in_frame = jnp.logical_or(
        jnp.logical_and(lane < HALF_LANES, q < 3), jnp.logical_and(lane >= HALF_LANES, q > 0)
    )

    def clip(value):
        return jnp.concatenate([value[:, :block], jnp.where(in_frame, value[:, block:], 0.0)], axis=1)

    def step(index):
        return 0 if index is None else 2 * index

    def edge_copy(name, side, field, index):
        if side == "inner":
            src, dst, tile = edge * (2 - core), 3 * edge * core, t
        else:
            src, dst, tile = edge * (1 + core), 3 * edge * (1 - core), outer_tile
        lead = (1,) if index is None else (1, index)
        return remote(
            field.at[lead + (pl.ds(src, edge),)], field.at[lead + (pl.ds(dst, edge),)],
            SEND[name, side] + step(index), RECV[name, side] + step(index), partner, tile,
        )

    def edge_in(name, side, field, index):
        if side == "inner":
            at, tile = 3 * edge * (1 - core), t
        else:
            at, tile = 3 * edge * core, outer_tile
        lead = (1,) if index is None else (1, index)
        piece = field.at[lead + (pl.ds(at, edge),)]
        return remote(piece, piece, SEND[name, side] + step(index), RECV[name, side] + step(index), partner, tile), at

    def send_edge(name, side, field, index=None):
        if side == "inner":
            edge_copy(name, side, field, index).start()
        else:
            @pl.when(has_outer)
            def _():
                edge_copy(name, side, field, index).start()

    def edge_sent(name, field, index=None):
        edge_copy(name, "inner", field, index).wait_send()

        @pl.when(has_outer)
        def _():
            edge_copy(name, "outer", field, index).wait_send()

    def turn(field, lead, at, count):
        for k in range(count):
            value = field[(1,) + lead + (at + k,)]
            field[(0,) + lead + (at + k,)] = pltpu.roll(value, 1, 1)
            field[(2,) + lead + (at + k,)] = pltpu.roll(value, span - 1, 1)

    hidden = (a_ref, c_ref, d_ref)

    def plan(counts, outer_phase):
        if outer_phase:
            return [(layer, i, 1) for layer in range(layers) for i in range(2)]
        steps = []
        for layer, count in enumerate(counts):
            offset = 0
            while offset < count:
                size = 2 if 2 * layer < layers and offset + 4 <= count else 1
                steps.append((layer, offset, size))
                offset += 2 * size
        return steps

    def network(read, w_ref, base, finish, outer_phase, before_last=None):
        accs = (acc0, acc1)
        totals = [2 * rows - 2 * (layer + 1) for layer in range(layers)]
        waiting = None
        for index, (layer, offset, size) in enumerate(plan([total - edge for total in totals], outer_phase)):
            last = layer == layers - 1
            if outer_phase:
                j = core * (totals[layer] - edge) + (2 * core if offset else 2 - 2 * core)
                clash = False
            else:
                j = edge * (1 - core) + offset
                clash = (
                    waiting is not None and waiting[1] < layer
                    and waiting[2] < offset + 2 * size + 2 and offset < waiting[2] + 2 * waiting[3]
                )
            if last and before_last is not None:
                before_last()
                before_last = None
            if clash:
                waiting[0]()
                waiting = None
            acc = accs[index % 2]
            source = read if layer == 0 else (lambda s, at, ref=hidden[layer - 1]: ref[s, at])
            stack = jnp.concatenate([
                jnp.concatenate(
                    [source(s, pl.ds(j + 2 * k, 4)).reshape(4 * channels, span) for k in range(size)], axis=1
                )
                for s in range(3)
            ], axis=0)
            acc[:, : size * span] = jnp.dot(w_ref[layer], stack, preferred_element_type=jnp.float32)
            if waiting is not None:
                waiting[0]()

            def post(acc=acc, j=j, layer=layer, last=last, size=size, offset=offset):
                shift = jnp.concatenate([bias[base + layer]] * (span // LANES), axis=1)
                for k in range(size):
                    value = acc[:, k * span : (k + 1) * span] + shift
                    if last:
                        finish(j + 2 * k, value)
                        continue
                    value = jnp.maximum(value, 0.0)
                    if outer_phase:
                        halves = []
                        for p in range(2):
                            outside = jnp.logical_and(
                                jnp.logical_not(has_outer),
                                jnp.logical_or(
                                    jnp.logical_and(is_even, 2 * (1 - offset) + p < layers - 1 - layer),
                                    jnp.logical_and(is_odd, 2 * offset + p > layer),
                                ),
                            )
                            halves.append(jnp.where(outside, 0.0, value[p * channels : (p + 1) * channels]))
                        value = jnp.concatenate(halves, axis=0)
                    emit(hidden[layer], (), j + 2 * k, value)

            waiting = post, layer, offset, size
        waiting[0]()

    def emit(ref, lead, j, value, versions=(0, 1, 2)):
        packed = clip(value).astype(jnp.bfloat16)
        for v in versions:
            turned = packed if v == 1 else pltpu.roll(packed, 1 if v == 0 else span - 1, 1)
            for p in range(2):
                ref[(v,) + lead + (j + p,)] = turned[p * channels : (p + 1) * channels]

    def pair_of(values):
        return jnp.concatenate([values[0], values[1]], axis=0).astype(jnp.float32)

    def field_network(name, field, index, w_ref, base, finish, after_inner, before_last=None):
        lead = () if index is None else (index,)
        read = lambda s, at: field[(s,) + lead + (at,)]
        copy, at = edge_in(name, "inner", field, index)
        copy.wait_recv()
        turn(field, lead, at, edge)
        network(read, w_ref, base, finish, False, before_last)
        after_inner()
        copy, at = edge_in(name, "outer", field, index)

        @pl.when(has_outer)
        def _():
            copy.wait_recv()
            turn(field, lead, at, edge)

        network(read, w_ref, base, finish, True)

    def out_copy(name, half, source, frame, dx, d):
        at = edge * (1 - core) if half == 0 else edge * core
        dy = flip(y, core)
        src = source(at)
        dst = out.at[pl.ds(at, edge), :, cols(q)]
        return remote(src, dst, SEND[name, half] + 2 * d, RECV["out", 0] + 4 * dx + 2 * dy + half, frame, first_tile + core), (
            lambda: pltpu.make_async_copy(src, dst, local_sem.at[5 + half])
        )

    def deliver(name, half, source, frame, dx, action, d=0):
        copy, local = out_copy(name, half, source, frame, dx, d)
        mine_only = jnp.logical_and(f == frame, me_local)

        @pl.when(jnp.logical_not(mine_only))
        def _():
            action(copy)

        @pl.when(mine_only)
        def _():
            action(local())

    def high_piece(d):
        return lambda at: h.at[1, d, pl.ds(edge + at, edge), :, 0:block]

    turn(e, (0,), edge, rows)
    send_edge("e0", "inner", e, 0)
    send_edge("e0", "outer", e, 0)
    def pair_network(d, carry):
        p_index = flip(x, d)

        @pl.when(d == 1)
        def _():
            arrive(0, 1)
            send_edge("e0", "inner", e, d)
            send_edge("e0", "outer", e, d)
            turn(e, (d,), edge, rows)

        def high(j, value):
            old = pair_of([o[d, j], o[d, j + 1]])
            emit(h, (d,), edge + j, old - value)

        def high_inner():
            send_edge("h0", "inner", h, d)

            @pl.when(d == 1)
            def _():
                deliver("high0", 0, high_piece(d), 2 * p_index + 1, d, start, d)

        def high_ready():
            for dx in range(2):
                @pl.when(d == dx)
                def _(dx=dx):
                    arrive(1, dx)
                    if dx:
                        for half in range(2):
                            deliver("high0", half, high_piece(0), 2 * x + 1, 0, start, 0)

        field_network("e0", e, d, wa, 0, high, high_inner, high_ready)
        send_edge("h0", "outer", h, d)

        @pl.when(d == 1)
        def _():
            deliver("high0", 1, high_piece(d), 2 * p_index + 1, d, start, d)


        def low(j, value):
            old = pair_of([e[1, d, edge + j], e[1, d, edge + j + 1]])
            packed = clip(old + value).astype(jnp.bfloat16)
            for v in range(3):
                turned = packed if v == 1 else pltpu.roll(packed, 1 if v == 0 else span - 1, 1)
                for p in range(2):
                    fb[p_index, v, edge + j + p] = turned[p * channels : (p + 1) * channels]

        def low_inner():
            @pl.when(x == d)
            def _():
                send_edge("f", "inner", fb.at[0])

        field_network("h0", h, d, wb, layers, low, low_inner)

        @pl.when(x == d)
        def _():
            send_edge("f", "outer", fb.at[0])

        return carry

    lax.fori_loop(0, 2, pair_network, 0)

    def high_two(j, value):
        old = pair_of([fb[1, 1, edge + j], fb[1, 1, edge + j + 1]])
        emit(g2, (), edge + j, old - value)

    def g_piece(at):
        return g2.at[1, pl.ds(edge + at, edge), :, 0:block]

    def g_inner():
        send_edge("g", "inner", g2)
        deliver("high2", 0, g_piece, 2, 1 - x, start)

    field_network("f", fb.at[0], None, wc, 2 * layers, high_two, g_inner)
    send_edge("g", "outer", g2)
    deliver("high2", 1, g_piece, 2, 1 - x, start)

    def low_two(j, value):
        old = pair_of([fb[0, 1, edge + j], fb[0, 1, edge + j + 1]])
        packed = (old + value)[:, :block].astype(jnp.bfloat16)
        for p in range(2):
            l2[j + p] = packed[p * channels : (p + 1) * channels]

    def l_piece(at):
        return l2.at[pl.ds(at, edge)]

    def l_inner():
        deliver("low2", 0, l_piece, 0, x, start)

    field_network("g", g2, None, wd, 3 * layers, low_two, l_inner)
    deliver("low2", 1, l_piece, 0, x, start)

    for dx in range(2):
        for dy in range(2):
            for half in range(2):
                rows_at = edge * (1 - y) if half == 0 else edge * y
                dst = out.at[pl.ds(rows_at, edge), :, cols(2 * flip(x, dx) + flip(y, dy))]
                copy = remote(dst, dst, 0, RECV["out", 0] + 4 * dx + 2 * dy + half, partner, t)
                if dx or dy:
                    copy.wait_recv()
                else:
                    @pl.when(jnp.logical_not(me_local))
                    def _(copy=copy):
                        copy.wait_recv()

                    @pl.when(me_local)
                    def _(dst=dst, half=half):
                        pltpu.make_async_copy(dst, dst, local_sem.at[5 + half]).wait()

    for c, flag in ((0, is_even), (1, is_odd)):
        @pl.when(flag)
        def _(c=c):
            for peer in PEERS:
                for part in ("main", "pad"):
                    ship(c, peer, part, settle)
    for d in range(2):
        edge_sent("e0", e, d)
        edge_sent("h0", h, d)
        for half in range(2):
            deliver("high0", half, high_piece(d), 2 * flip(x, d) + 1, d, settle, d)
    edge_sent("f", fb.at[0])
    edge_sent("g", g2)
    for half in range(2):
        deliver("high2", half, g_piece, 2, 1 - x, settle)
        deliver("low2", half, l_piece, 0, x, settle)


def local(frames, predict_w, predict_b, update_w, update_b):
    own = jnp.transpose(frames[0], (1, 0, 2))
    rows, channels, width = own.shape
    layers = predict_w.shape[1]
    block = width // 4
    span = block + LANES
    packed = rows * 8 * layers // LANES
    tiles = lax.axis_size("tile")
    vmem = pl.BlockSpec(memory_space=pltpu.VMEM)
    hbm = pl.BlockSpec(memory_space=pl.ANY)

    def buffer(*lead, columns=span):
        return pltpu.VMEM(lead + (channels, columns), jnp.bfloat16)

    weight = pltpu.VMEM((layers, 2 * channels, 12 * channels), jnp.bfloat16)
    acc = pltpu.VMEM((2 * channels, 2 * span), jnp.float32)
    result = pl.pallas_call(
        functools.partial(kernel, tiles),
        out_shape=jax.ShapeDtypeStruct(own.shape, jnp.bfloat16),
        in_specs=[hbm, vmem, vmem, vmem, vmem],
        out_specs=hbm,
        scratch_shapes=[
            buffer(3, 2, 2 * rows), buffer(2, rows), buffer(3, 2, 2 * rows), buffer(2, 3, 2 * rows),
            buffer(3, 2 * rows), buffer(rows, columns=block),
            buffer(3, 2 * rows - 2), buffer(3, 2 * rows - 4), buffer(3, 2 * rows - 6),
            acc, acc, weight, weight, weight, weight,
            pltpu.VMEM((4 * layers, 2 * channels, LANES), jnp.float32),
            buffer(3, rows, columns=2 * LANES), buffer(4, packed, columns=LANES), buffer(2, 2, packed, columns=LANES),
            pltpu.SemaphoreType.DMA((len(SEND),)),
            pltpu.SemaphoreType.DMA((len(RECV),)),
            pltpu.SemaphoreType.DMA((7,)),
        ],
        compiler_params=pltpu.CompilerParams(
            collective_id=0, has_side_effects=True, vmem_limit_bytes=60 * 1024 * 1024
        ),
    )(own, predict_w, update_w, predict_b, update_b)
    return jnp.transpose(result, (1, 0, 2))[None]


def solution(mesh):
    in_specs = (P("frame", None, "tile", None), P(), P(), P(), P())
    out_specs = P("frame", None, "tile", None)
    return jax.shard_map(local, mesh=mesh, in_specs=in_specs, out_specs=out_specs, check_vma=False)
```

```python
import functools

import jax
import jax.numpy as jnp
from jax import lax
from jax.experimental import pallas as pl
from jax.experimental.pallas import tpu as pltpu
from jax.sharding import PartitionSpec as P

LANES = 128
HALF_LANES = LANES // 2
PEERS = ((0, 1), (1, 0), (1, 1), (0, 0))
EDGES = ("e0", "e1", "h0", "h1", "f", "g")
RECV, SEND = {}, {}
for _kind in ("main", "pad"):
    for _c in range(2):
        for _dx in range(2):
            RECV[_kind, _c, _dx] = len(RECV)
for _k in range(8):
    RECV["out", _k] = len(RECV)
for _e in EDGES:
    for _side in ("inner", "outer"):
        RECV[_e, _side] = len(RECV)
for _kind in ("main", "pad"):
    for _p in PEERS:
        SEND[_kind, _p] = len(SEND)
for _name in ("high0", "high1", "high2", "low2"):
    for _k in range(2):
        SEND[_name, _k] = len(SEND)
for _e in EDGES:
    for _side in ("inner", "outer"):
        SEND[_e, _side] = len(SEND)


def flip(v, d):
    return v + d - 2 * v * d


def kernel(tiles, own, pw_in, uw_in, pb, ub, out, pw, uw, e, o, h, fb, g2, l2, a_ref, c_ref, d_ref, acc0, acc1, wa, wb, wc, wd,
           bias, cuts, pads, packs, send_sem, recv_sem, local_sem):
    rows, channels, width = own.shape
    layers = pw.shape[1]
    block = width // 4
    span = block + LANES
    edge = rows // 2
    f = lax.axis_index("frame")
    t = lax.axis_index("tile")
    core, x = lax.rem(f, 2), lax.div(f, 2)
    y, slab = lax.rem(t, 2), lax.div(t, 2)
    slabs = tiles // 2
    first_tile = t - y
    partner = f + 1 - 2 * core
    q = 2 * x + y
    is_even, is_odd = core == 0, core == 1
    outer_slab = slab + 2 * core - 1
    has_outer = jnp.logical_and(outer_slab >= 0, outer_slab < slabs)
    outer_tile = t + 4 * core - 2
    me_local = y == core

    def cols(k, size=block):
        return pl.ds(pl.multiple_of(k * block, LANES), size)

    barrier = pltpu.get_barrier_semaphore()

    def greet(frame, tile):
        pl.semaphore_signal(
            barrier, inc=1, device_id={"frame": frame, "tile": tile}, device_id_type=pl.DeviceIdType.MESH,
        )

    for dx in range(2):
        for dc in range(2):
            for dy in range(2):
                if dx or dc or dy:
                    greet(2 * flip(x, dx) + flip(core, dc), first_tile + flip(y, dy))

    @pl.when(has_outer)
    def _():
        greet(partner, outer_tile)

    def remote(src, dst, send, recv, frame, tile):
        return pltpu.make_async_remote_copy(
            src_ref=src, dst_ref=dst, send_sem=send_sem.at[send], recv_sem=recv_sem.at[recv],
            device_id={"frame": frame, "tile": tile}, device_id_type=pl.DeviceIdType.MESH,
        )

    cut_copies = [
        pltpu.make_async_copy(
            own.at[:, :, k * block + block - LANES : k * block + block + LANES], cuts.at[k], local_sem.at[k]
        )
        for k in range(3)
    ]
    weight_copies = [
        pltpu.make_async_copy(src, dst, local_sem.at[7 + k]) for k, (src, dst) in enumerate(((pw_in, pw), (uw_in, uw)))
    ]
    for copy in cut_copies + weight_copies:
        copy.start()

    pl.semaphore_wait(barrier, 7 + has_outer.astype(jnp.int32))

    mine = slice(edge, edge + rows)
    reach = 4 * layers
    group = LANES // (2 * reach)

    def landing(c, dx, part):
        if part == "pad":
            return packs.at[c, dx]
        return e.at[1, dx, mine, :, 0:block] if c == 0 else o.at[dx, :, :, 0:block]

    def parcel(c, peer, part):
        dx, dy = peer
        px, py = flip(x, dx), flip(y, dy)
        pq = 2 * px + py
        src = own.at[:, :, cols(pq)] if part == "main" else pads.at[pq]
        return src, landing(c, dx, part), 2 * px + y, first_tile + py

    def ship(c, peer, part, action):
        src, dst, frame, tile = parcel(c, peer, part)
        copy = remote(src, dst, SEND[part, peer], RECV[part, c, peer[0]], frame, tile)
        if peer != (0, 0):
            action(copy)
        else:
            same = y == c

            @pl.when(jnp.logical_not(same))
            def _():
                action(copy)

            @pl.when(same)
            def _():
                action(pltpu.make_async_copy(src, dst, local_sem.at[3 if part == "main" else 4]))

    def start(copy):
        copy.start()

    def settle(copy):
        if copy.is_remote:
            copy.wait_send()

    def arrive(c, dx):
        for part in ("main", "pad"):
            src, dst, frame, tile = parcel(c, (dx, 0), part)
            copy = remote(src, dst, SEND[part, (dx, 0)], RECV[part, c, dx], frame, tile)
            if dx:
                copy.wait_recv()
            else:
                local = jnp.logical_and(me_local, core == c)

                @pl.when(jnp.logical_not(local))
                def _(copy=copy):
                    copy.wait_recv()

                @pl.when(local)
                def _(src=src, dst=dst, part=part):
                    pltpu.make_async_copy(src, dst, local_sem.at[3 if part == "main" else 4]).wait()
        for unit in range(rows // group):
            value = packs[c, dx, unit].astype(jnp.float32)
            for i in range(group):
                strip = pltpu.roll(value, (-reach - 2 * reach * i) % LANES, 1)
                strip = jnp.where(jnp.logical_or(lane < reach, lane >= LANES - reach), strip, 0.0).astype(jnp.bfloat16)
                row = unit * group + i
                if c == 0:
                    e[1, dx, edge + row, :, block:span] = strip
                else:
                    o[dx, row, :, block:span] = strip

    @pl.when(is_even)
    def _():
        for peer in ((0, 1), (1, 0), (0, 0)):
            ship(0, peer, "main", start)

    @pl.when(is_odd)
    def _():
        for peer in ((0, 1), (1, 0), (0, 0)):
            ship(1, peer, "main", start)

    lane = lax.broadcasted_iota(jnp.int32, (1, LANES), 1)
    for copy in cut_copies:
        copy.wait()
    for k in range(4):
        for unit in range(rows // group):
            total = jnp.zeros((channels, LANES), jnp.float32)
            for i in range(group):
                row = unit * group + i
                strip = jnp.zeros((channels, LANES), jnp.float32)
                if k < 3:
                    strip = jnp.where(lane < reach, cuts[k, row, :, LANES:].astype(jnp.float32), strip)
                if k > 0:
                    strip = jnp.where(lane >= LANES - reach, cuts[k - 1, row, :, :LANES].astype(jnp.float32), strip)
                total = total + pltpu.roll(strip, (reach + 2 * reach * i) % LANES, 1)
            pads[k, unit] = total.astype(jnp.bfloat16)

    @pl.when(is_even)
    def _():
        for peer in ((0, 1), (1, 0), (0, 0)):
            ship(0, peer, "pad", start)
        for part in ("main", "pad"):
            ship(0, (1, 1), part, start)

    @pl.when(is_odd)
    def _():
        for peer in ((0, 1), (1, 0), (0, 0)):
            ship(1, peer, "pad", start)
        for part in ("main", "pad"):
            ship(1, (1, 1), part, start)

    def build(k_ref, level, w_ref):
        for layer in range(layers):
            w_ref[layer] = jnp.zeros(w_ref.shape[1:], w_ref.dtype)
            for p in range(2):
                for s in range(3):
                    for r in range(3):
                        at = 4 * channels * s + channels * (r + p)
                        w_ref[layer, p * channels : (p + 1) * channels, at : at + channels] = k_ref[level, layer, r, s]

    def spread_bias(b_ref, level, base):
        row = lax.broadcasted_iota(jnp.int32, (channels, channels), 0)
        col = lax.broadcasted_iota(jnp.int32, (channels, channels), 1)
        for layer in range(layers):
            values = jnp.where(row == col, b_ref[level, layer : layer + 1, :], 0.0)
            column = jnp.sum(values, axis=1, keepdims=True)
            full = jnp.broadcast_to(column, (channels, LANES))
            bias[base + layer, :channels] = full
            bias[base + layer, channels:] = full

    @pl.when(jnp.logical_not(has_outer))
    def _():
        zero = jnp.zeros((edge, channels, span), jnp.bfloat16)
        at = pl.ds(3 * edge * core, edge)
        for v in range(3):
            for d in range(2):
                e[v, d, at] = zero
                h[v, d, at] = zero
            fb[0, v, at] = zero
            g2[v, at] = zero

    for copy in weight_copies:
        copy.wait()
    for k, (k_ref, b_ref, level, w_ref) in enumerate(
        ((pw, pb, 0, wa), (uw, ub, 0, wb), (pw, pb, 1, wc), (uw, ub, 1, wd))
    ):
        build(k_ref, level, w_ref)
        spread_bias(b_ref, level, k * layers)
    arrive(0, 0)

    in_frame = jnp.logical_or(
        jnp.logical_and(lane < HALF_LANES, q < 3), jnp.logical_and(lane >= HALF_LANES, q > 0)
    )

    def clip(value):
        return jnp.concatenate([value[:, :block], jnp.where(in_frame, value[:, block:], 0.0)], axis=1)

    def step(index):
        return 0 if index is None else 2 * index

    def edge_copy(name, side, field, index):
        if side == "inner":
            src, dst, tile = edge * (2 - core), 3 * edge * core, t
        else:
            src, dst, tile = edge * (1 + core), 3 * edge * (1 - core), outer_tile
        lead = (1,) if index is None else (1, index)
        return remote(
            field.at[lead + (pl.ds(src, edge),)], field.at[lead + (pl.ds(dst, edge),)],
            SEND[name, side] + step(index), RECV[name, side] + step(index), partner, tile,
        )

    def edge_in(name, side, field, index):
        if side == "inner":
            at, tile = 3 * edge * (1 - core), t
        else:
            at, tile = 3 * edge * core, outer_tile
        lead = (1,) if index is None else (1, index)
        piece = field.at[lead + (pl.ds(at, edge),)]
        return remote(piece, piece, SEND[name, side] + step(index), RECV[name, side] + step(index), partner, tile), at

    def send_edge(name, side, field, index=None):
        if side == "inner":
            edge_copy(name, side, field, index).start()
        else:
            @pl.when(has_outer)
            def _():
                edge_copy(name, side, field, index).start()

    def edge_sent(name, field, index=None):
        edge_copy(name, "inner", field, index).wait_send()

        @pl.when(has_outer)
        def _():
            edge_copy(name, "outer", field, index).wait_send()

    def turn(field, lead, at, count):
        for k in range(count):
            value = field[(1,) + lead + (at + k,)]
            field[(0,) + lead + (at + k,)] = pltpu.roll(value, 1, 1)
            field[(2,) + lead + (at + k,)] = pltpu.roll(value, span - 1, 1)

    hidden = (a_ref, c_ref, d_ref)

    def plan(counts, outer_phase):
        if outer_phase:
            return [(layer, i, 1) for layer in range(layers) for i in range(2)]
        steps = []
        for layer, count in enumerate(counts):
            offset = 0
            while offset < count:
                size = 2 if 2 * layer < layers and offset + 4 <= count else 1
                steps.append((layer, offset, size))
                offset += 2 * size
        return steps

    def network(read, w_ref, base, finish, outer_phase, before_last=None):
        accs = (acc0, acc1)
        totals = [2 * rows - 2 * (layer + 1) for layer in range(layers)]
        waiting = None
        for index, (layer, offset, size) in enumerate(plan([total - edge for total in totals], outer_phase)):
            last = layer == layers - 1
            if outer_phase:
                j = core * (totals[layer] - edge) + (2 * core if offset else 2 - 2 * core)
                clash = False
            else:
                j = edge * (1 - core) + offset
                clash = (
                    waiting is not None and waiting[1] < layer
                    and waiting[2] < offset + 2 * size + 2 and offset < waiting[2] + 2 * waiting[3]
                )
            if last and before_last is not None:
                before_last()
                before_last = None
            if clash:
                waiting[0]()
                waiting = None
            acc = accs[index % 2]
            source = read if layer == 0 else (lambda s, at, ref=hidden[layer - 1]: ref[s, at])
            stack = jnp.concatenate([
                jnp.concatenate(
                    [source(s, pl.ds(j + 2 * k, 4)).reshape(4 * channels, span) for k in range(size)], axis=1
                )
                for s in range(3)
            ], axis=0)
            acc[:, : size * span] = jnp.dot(w_ref[layer], stack, preferred_element_type=jnp.float32)
            if waiting is not None:
                waiting[0]()

            def post(acc=acc, j=j, layer=layer, last=last, size=size, offset=offset):
                shift = jnp.concatenate([bias[base + layer]] * (span // LANES), axis=1)
                for k in range(size):
                    value = acc[:, k * span : (k + 1) * span] + shift
                    if last:
                        finish(j + 2 * k, value)
                        continue
                    value = jnp.maximum(value, 0.0)
                    if outer_phase:
                        halves = []
                        for p in range(2):
                            outside = jnp.logical_and(
                                jnp.logical_not(has_outer),
                                jnp.logical_or(
                                    jnp.logical_and(is_even, 2 * (1 - offset) + p < layers - 1 - layer),
                                    jnp.logical_and(is_odd, 2 * offset + p > layer),
                                ),
                            )
                            halves.append(jnp.where(outside, 0.0, value[p * channels : (p + 1) * channels]))
                        value = jnp.concatenate(halves, axis=0)
                    emit(hidden[layer], (), j + 2 * k, value)

            waiting = post, layer, offset, size
        waiting[0]()

    def emit(ref, lead, j, value, versions=(0, 1, 2)):
        packed = clip(value).astype(jnp.bfloat16)
        for v in versions:
            turned = packed if v == 1 else pltpu.roll(packed, 1 if v == 0 else span - 1, 1)
            for p in range(2):
                ref[(v,) + lead + (j + p,)] = turned[p * channels : (p + 1) * channels]

    def pair_of(values):
        return jnp.concatenate([values[0], values[1]], axis=0).astype(jnp.float32)

    def field_network(name, field, index, w_ref, base, finish, after_inner, before_last=None):
        lead = () if index is None else (index,)
        read = lambda s, at: field[(s,) + lead + (at,)]
        copy, at = edge_in(name, "inner", field, index)
        copy.wait_recv()
        turn(field, lead, at, edge)
        network(read, w_ref, base, finish, False, before_last)
        after_inner()
        copy, at = edge_in(name, "outer", field, index)

        @pl.when(has_outer)
        def _():
            copy.wait_recv()
            turn(field, lead, at, edge)

        network(read, w_ref, base, finish, True)

    def out_copy(name, half, source, frame, dx, d):
        at = edge * (1 - core) if half == 0 else edge * core
        dy = flip(y, core)
        src = source(at)
        dst = out.at[pl.ds(at, edge), :, cols(q)]
        return remote(src, dst, SEND[name, half] + 2 * d, RECV["out", 0] + 4 * dx + 2 * dy + half, frame, first_tile + core), (
            lambda: pltpu.make_async_copy(src, dst, local_sem.at[5 + half])
        )

    def deliver(name, half, source, frame, dx, action, d=0):
        copy, local = out_copy(name, half, source, frame, dx, d)
        mine_only = jnp.logical_and(f == frame, me_local)

        @pl.when(jnp.logical_not(mine_only))
        def _():
            action(copy)

        @pl.when(mine_only)
        def _():
            action(local())

    def high_piece(d):
        return lambda at: h.at[1, d, pl.ds(edge + at, edge), :, 0:block]

    turn(e, (0,), edge, rows)
    send_edge("e0", "inner", e, 0)
    send_edge("e0", "outer", e, 0)
    def pair_network(d, carry):
        p_index = flip(x, d)

        def high(j, value):
            old = pair_of([o[d, j], o[d, j + 1]])
            emit(h, (d,), edge + j, old - value)

        def high_inner():
            send_edge("h0", "inner", h, d)

            @pl.when(d == 1)
            def _():
                deliver("high0", 0, high_piece(d), 2 * p_index + 1, d, start, d)

        def high_ready():
            for dx in range(2):
                @pl.when(d == dx)
                def _(dx=dx):
                    arrive(1, dx)
                    if dx:
                        for half in range(2):
                            deliver("high0", half, high_piece(0), 2 * x + 1, 0, start, 0)

        field_network("e0", e, d, wa, 0, high, high_inner, high_ready)
        send_edge("h0", "outer", h, d)

        @pl.when(d == 1)
        def _():
            deliver("high0", 1, high_piece(d), 2 * p_index + 1, d, start, d)


        def low(j, value):
            old = pair_of([e[1, d, edge + j], e[1, d, edge + j + 1]])
            packed = clip(old + value).astype(jnp.bfloat16)
            for v in range(3):
                turned = packed if v == 1 else pltpu.roll(packed, 1 if v == 0 else span - 1, 1)
                for p in range(2):
                    fb[p_index, v, edge + j + p] = turned[p * channels : (p + 1) * channels]

        def low_inner():
            @pl.when(x == d)
            def _():
                send_edge("f", "inner", fb.at[0])

            @pl.when(d == 0)
            def _():
                arrive(0, 1)
                send_edge("e0", "inner", e, 1)
                send_edge("e0", "outer", e, 1)
                turn(e, (1,), edge, rows)

        field_network("h0", h, d, wb, layers, low, low_inner)

        @pl.when(x == d)
        def _():
            send_edge("f", "outer", fb.at[0])

        return carry

    lax.fori_loop(0, 2, pair_network, 0)

    def high_two(j, value):
        old = pair_of([fb[1, 1, edge + j], fb[1, 1, edge + j + 1]])
        emit(g2, (), edge + j, old - value)

    def g_piece(at):
        return g2.at[1, pl.ds(edge + at, edge), :, 0:block]

    def g_inner():
        send_edge("g", "inner", g2)
        deliver("high2", 0, g_piece, 2, 1 - x, start)

    field_network("f", fb.at[0], None, wc, 2 * layers, high_two, g_inner)
    send_edge("g", "outer", g2)
    deliver("high2", 1, g_piece, 2, 1 - x, start)

    def low_two(j, value):
        old = pair_of([fb[0, 1, edge + j], fb[0, 1, edge + j + 1]])
        packed = (old + value)[:, :block].astype(jnp.bfloat16)
        for p in range(2):
            l2[j + p] = packed[p * channels : (p + 1) * channels]

    def l_piece(at):
        return l2.at[pl.ds(at, edge)]

    def l_inner():
        deliver("low2", 0, l_piece, 0, x, start)

    field_network("g", g2, None, wd, 3 * layers, low_two, l_inner)
    deliver("low2", 1, l_piece, 0, x, start)

    for dx in range(2):
        for dy in range(2):
            for half in range(2):
                rows_at = edge * (1 - y) if half == 0 else edge * y
                dst = out.at[pl.ds(rows_at, edge), :, cols(2 * flip(x, dx) + flip(y, dy))]
                copy = remote(dst, dst, 0, RECV["out", 0] + 4 * dx + 2 * dy + half, partner, t)
                if dx or dy:
                    copy.wait_recv()
                else:
                    @pl.when(jnp.logical_not(me_local))
                    def _(copy=copy):
                        copy.wait_recv()

                    @pl.when(me_local)
                    def _(dst=dst, half=half):
                        pltpu.make_async_copy(dst, dst, local_sem.at[5 + half]).wait()

    for c, flag in ((0, is_even), (1, is_odd)):
        @pl.when(flag)
        def _(c=c):
            for peer in PEERS:
                for part in ("main", "pad"):
                    ship(c, peer, part, settle)
    for d in range(2):
        edge_sent("e0", e, d)
        edge_sent("h0", h, d)
        for half in range(2):
            deliver("high0", half, high_piece(d), 2 * flip(x, d) + 1, d, settle, d)
    edge_sent("f", fb.at[0])
    edge_sent("g", g2)
    for half in range(2):
        deliver("high2", half, g_piece, 2, 1 - x, settle)
        deliver("low2", half, l_piece, 0, x, settle)


def local(frames, predict_w, predict_b, update_w, update_b):
    own = jnp.transpose(frames[0], (1, 0, 2))
    rows, channels, width = own.shape
    layers = predict_w.shape[1]
    block = width // 4
    span = block + LANES
    packed = rows * 8 * layers // LANES
    tiles = lax.axis_size("tile")
    vmem = pl.BlockSpec(memory_space=pltpu.VMEM)
    hbm = pl.BlockSpec(memory_space=pl.ANY)

    def buffer(*lead, columns=span):
        return pltpu.VMEM(lead + (channels, columns), jnp.bfloat16)

    weight = pltpu.VMEM((layers, 2 * channels, 12 * channels), jnp.bfloat16)
    acc = pltpu.VMEM((2 * channels, 2 * span), jnp.float32)
    result = pl.pallas_call(
        functools.partial(kernel, tiles),
        out_shape=jax.ShapeDtypeStruct(own.shape, jnp.bfloat16),
        in_specs=[hbm, hbm, hbm, vmem, vmem],
        out_specs=hbm,
        scratch_shapes=[
            pltpu.VMEM(predict_w.shape, predict_w.dtype), pltpu.VMEM(update_w.shape, update_w.dtype),
            buffer(3, 2, 2 * rows), buffer(2, rows), buffer(3, 2, 2 * rows), buffer(2, 3, 2 * rows),
            buffer(3, 2 * rows), buffer(rows, columns=block),
            buffer(3, 2 * rows - 2), buffer(3, 2 * rows - 4), buffer(3, 2 * rows - 6),
            acc, acc, weight, weight, weight, weight,
            pltpu.VMEM((4 * layers, 2 * channels, LANES), jnp.float32),
            buffer(3, rows, columns=2 * LANES), buffer(4, packed, columns=LANES), buffer(2, 2, packed, columns=LANES),
            pltpu.SemaphoreType.DMA((len(SEND),)),
            pltpu.SemaphoreType.DMA((len(RECV),)),
            pltpu.SemaphoreType.DMA((9,)),
        ],
        compiler_params=pltpu.CompilerParams(
            collective_id=0, has_side_effects=True, vmem_limit_bytes=60 * 1024 * 1024
        ),
    )(own, predict_w, update_w, predict_b, update_b)
    return jnp.transpose(result, (1, 0, 2))[None]


def solution(mesh):
    in_specs = (P("frame", None, "tile", None), P(), P(), P(), P())
    out_specs = P("frame", None, "tile", None)
    return jax.shard_map(local, mesh=mesh, in_specs=in_specs, out_specs=out_specs, check_vma=False)
```
